32 devices in a mesh: px: 4 (over x, core), py: 8 (over z, y).
Axes of the slice: x: 2, y: 2, z: 4, core: 2. Of those that a mesh axis runs over, the one named last changes fastest.
Arguments:
- field: float32 [256, 256, 256], P('px', 'py'), may hold values from -6 to 6
- diffusivity: bfloat16 [256, 256, 256], P('px', 'py'), may hold values from 0.049804688 to 1
- velocity: bfloat16 [3, 256, 256, 256], P(None, 'px', 'py'), may hold values from -4 to 4
- margin: int32 [4, 2], P('px'), may hold values from 0 to 4, as said below
Outputs:
- advected: float32 [256, 256, 256], P('px', 'py')
- controls: float32 [128, 128, 128], P('px', 'py')
The draws below stay inside these ranges and needn't reach their ends.
Inputs may be any that keep to these rules, and one draw needn't show every extreme that they name: One subdomain has an upper margin of 0 and one has a lower margin of 4.
All inputs are finite; a program needn't handle non-finite values.
Results may differ from the reference program's by a relative error of at most 0.0003.
Values may be sent and summed in bfloat16 or wider, within the bound.
A program may use at most 192 MiB of HBM per device.

```python
import math
import jax
import jax.numpy as jnp
from jax import lax

CX = 64
NZ = 256
STEPS = 4
SWEEPS = 2
OVMAX = 4
NX = 256
NY = 256
N_PX = 4


def draw_margin(key, part):
    first_key, second_key, third_key = jax.random.split(jax.random.fold_in(key, 71), 3)
    values = jax.random.randint(first_key, (N_PX, 2), 0, OVMAX + 1)
    lower_owner = jax.random.randint(second_key, (), 0, N_PX)
    upper_owner = jax.random.randint(third_key, (), 0, N_PX)
    values = values.at[lower_owner, 0].set(OVMAX)
    values = values.at[upper_owner, 1].set(0)
    return values.astype(jnp.int32)


def steps_of(stream_key, dims, cuts, smallest, largest):
    def one(axis_at, parts):
        steps = jax.random.uniform(jax.random.fold_in(jax.random.fold_in(stream_key, 6), axis_at), (parts,), jnp.float32, smallest / len(cuts), largest / len(cuts))
        return jnp.repeat(jnp.exp(steps), dims[axis_at] // parts).reshape((-1,) + (1,) * (len(dims) - axis_at - 1))

    factor_of = one(*cuts[0])
    for cut in cuts[1:]:
        factor_of = factor_of * one(*cut)
    return factor_of


def scatter_about(own_key, shape, spread, limit, shards=(), kind=jnp.bfloat16):
    factor_of = steps_of(own_key, shape, shards, -0.22, 0.18) if shards else 1.0
    result = jax.random.normal(own_key, shape, jnp.float32) * spread * factor_of
    return jnp.minimum(jnp.maximum(result, -limit), limit).astype(kind)


def setup_inputs(seed: int = 0) -> dict:
    key_of = jax.random.split(jax.random.key(seed), 5)
    return {
        "field": scatter_about(key_of[0], (NX, NY, NZ), 1.0, 6.0, ((0, 4), (1, 8)), jnp.float32),
        "diffusivity": jnp.clip(jnp.exp(math.log(1.0) - 2.9996462 * jax.random.uniform(key_of[1], (NX, NY, NZ), jnp.float32) ** steps_of(key_of[1], (NX, NY, NZ), ((0, 4), (1, 8)), -0.2, 0.2)), 0.049804688, 1.0).astype(jnp.bfloat16),
        "velocity": scatter_about(key_of[2], (3, NX, NY, NZ), 1.0, 4.0, ((1, 4), (2, 8))),
        "margin": draw_margin(jax.random.fold_in(key_of[4], 71), 0),
    }


HIGH = lax.Precision.HIGHEST

def bspline(offset):
    magnitude = jnp.abs(offset)
    inner_part = (4.0 - 6.0 * magnitude * magnitude + 3.0 * magnitude ** 3) / 6.0
    outer_part = jnp.maximum(2.0 - magnitude, 0.0) ** 3 / 6.0
    return jnp.where(magnitude < 1.0, inner_part, outer_part)

def basis(samples, knots, samp_total, ctrl_total):
    position = samples[:, None].astype(jnp.float32) - 2.0 * knots[None, :].astype(jnp.float32) - 0.5
    values = bspline(0.5 * position)
    valid = (samples[:, None] >= 0) & (samples[:, None] < samp_total) & (knots[None, :] >= 0) & (knots[None, :] < ctrl_total)
    return jnp.where(valid, values, 0.0)

def gram(row_knots, col_knots, first, count, samp_total, ctrl_total):
    window = first + jnp.arange(count, dtype=jnp.int32)
    left_basis = basis(window, row_knots, samp_total, ctrl_total)
    right_basis = basis(window, col_knots, samp_total, ctrl_total)
    return jnp.dot(left_basis.T.astype(jnp.float32), right_basis.astype(jnp.float32), precision=HIGH, preferred_element_type=jnp.float32)

def chol_solve(lower, rhs_block):
    middle = lax.linalg.triangular_solve(lower, rhs_block, left_side=True, lower=True)
    return lax.linalg.triangular_solve(lower, middle, left_side=True, lower=True, transpose_a=True)

def sub_gram(start, left, right, block, samp_total, ctrl_total):
    width = block + 2 * OVMAX
    knots = start - OVMAX + jnp.arange(width, dtype=jnp.int32)
    full = gram(knots, knots, 2 * (start - OVMAX) - 4, 2 * width + 8, samp_total, ctrl_total)
    inside = (knots >= start - left) & (knots < start + block + right) & (knots >= 0) & (knots < ctrl_total)
    weight = inside.astype(jnp.float32)
    return (full * weight[:, None] * weight[None, :] + jnp.diag(1.0 - weight), weight)

def inner(array, shift_x, shift_y, shift_z):
    size_x, size_y, size_z = array.shape[-3:]
    return array[..., 1 + shift_x:size_x - 1 + shift_x, 1 + shift_y:size_y - 1 + shift_y, 1 + shift_z:size_z - 1 + shift_z]

def update(padded, kappa_pad, velo_pad):
    centre = inner(padded, 0, 0, 0)
    kappa_mid = inner(kappa_pad, 0, 0, 0)
    flux = velo_pad * (0.5 * padded * padded)[None]
    tendency = jnp.zeros_like(centre)
    for axis_index in range(3):
        plus = [0, 0, 0]
        minus = [0, 0, 0]
        plus[axis_index] = 1
        minus[axis_index] = -1
        upper = inner(padded, *plus)
        lower = inner(padded, *minus)
        kappa_up = inner(kappa_pad, *plus)
        kappa_low = inner(kappa_pad, *minus)
        flux_up = inner(flux[axis_index], *plus)
        flux_low = inner(flux[axis_index], *minus)
        tendency = tendency + 0.5 * (kappa_mid + kappa_up) * (upper - centre) - 0.5 * (kappa_mid + kappa_low) * (centre - lower) - 0.5 * (flux_up - flux_low)
    return centre + 0.1 * tendency

def fit_matrix(samp_total):
    ctrl_total = samp_total // 2
    table = basis(jnp.arange(samp_total, dtype=jnp.int32), jnp.arange(ctrl_total, dtype=jnp.int32), samp_total, ctrl_total)
    normal = jnp.dot(table.T.astype(jnp.float32), table.astype(jnp.float32), precision=HIGH, preferred_element_type=jnp.float32)
    return chol_solve(jnp.linalg.cholesky(normal), table.T)

def reference(field, diffusivity, velocity, margin):
    size_x, size_y, size_z = field.shape
    kappa_pad = jnp.pad(diffusivity.astype(jnp.float32), 1)
    velo_pad = jnp.pad(velocity.astype(jnp.float32), ((0, 0), (1, 1), (1, 1), (1, 1)))
    current = field
    for step_index in range(STEPS):
        current = update(jnp.pad(current, 1), kappa_pad, velo_pad)
    advected = current
    z_fit = fit_matrix(size_z)
    zfit = jnp.einsum('xyz,mz->xym', advected, z_fit, precision=HIGH)
    y_fit = fit_matrix(size_y)
    yfit = jnp.einsum('my,xyz->xmz', y_fit, zfit, precision=HIGH)
    samples = yfit.reshape(size_x, -1)
    ctrl_x = size_x // 2
    x_table = basis(jnp.arange(size_x, dtype=jnp.int32), jnp.arange(ctrl_x, dtype=jnp.int32), size_x, ctrl_x)
    rhs_all = jnp.dot(x_table.T.astype(jnp.float32), samples.astype(jnp.float32), precision=HIGH, preferred_element_type=jnp.float32)
    gram_all = jnp.dot(x_table.T.astype(jnp.float32), x_table.astype(jnp.float32), precision=HIGH, preferred_element_type=jnp.float32)
    block = CX // 2
    fitted = jnp.zeros_like(rhs_all)
    for sweep_index in range(SWEEPS):
        resid = rhs_all - jnp.dot(gram_all.astype(jnp.float32), fitted.astype(jnp.float32), precision=HIGH, preferred_element_type=jnp.float32)
        pieces = []
        for owner in range(N_PX):
            start = owner * block
            local_gram, weight = sub_gram(start, margin[owner, 0], margin[owner, 1], block, size_x, ctrl_x)
            knots = start - OVMAX + jnp.arange(block + 2 * OVMAX, dtype=jnp.int32)
            local_rhs = resid[jnp.clip(knots, 0, ctrl_x - 1)] * weight[:, None]
            correct = chol_solve(jnp.linalg.cholesky(local_gram), local_rhs)
            pieces.append(correct[OVMAX:OVMAX + block])
        fitted = fitted + jnp.concatenate(pieces, axis=0)
    return (advected, fitted.reshape(ctrl_x, size_y // 2, size_z // 2))
```

```python
import functools

import jax
import jax.numpy as jnp
import numpy as np
from jax import lax
from jax.experimental import pallas as pl
from jax.experimental.pallas import tpu as pltpu
from jax.sharding import PartitionSpec as P

STEPS = 4
OVMAX = 4
HALO = 8
QROWS = 24
HIGH = lax.Precision.HIGHEST
MESH = pl.DeviceIdType.MESH


def bspline(t):
    t = np.abs(t)
    inner = (4.0 - 6.0 * t * t + 3.0 * t**3) / 6.0
    outer = np.maximum(2.0 - t, 0.0) ** 3 / 6.0
    return np.where(t < 1.0, inner, outer)


def basis(total):
    j = np.arange(total, dtype=np.float64)[:, None]
    k = np.arange(total // 2, dtype=np.float64)[None, :]
    return bspline(0.5 * (j - 2.0 * k - 0.5))


TAPS = [float(bspline(0.5 * (j - 3.5))) for j in range(8)]


def z_matrix(total):
    table = basis(total)
    return np.linalg.solve(table.T @ table, table.T).T.astype(np.float32)


def y_matrix(total, count):
    table = basis(total)
    inverse = np.linalg.inv(table.T @ table)
    ctrl = total // 2
    own = ctrl // count
    result = np.zeros((ctrl, count, QROWS))
    for p in range(count):
        for q in range(own + 4):
            k = own * p - 2 + q
            if 0 <= k < ctrl:
                result[:, p, q] = inverse[:, k]
    return result.reshape(ctrl, count * QROWS).astype(np.float32)


def schwarz_table(total, count):
    table = basis(total)
    gram = table.T @ table
    ctrl = total // 2
    block = ctrl // count
    width = block + 2 * OVMAX
    out = np.zeros((3, OVMAX + 1, OVMAX + 1, 2, block, block + 2 * HALO))
    for kind, p in enumerate((0, min(1, count - 1), count - 1)):
        start = p * block
        knots = start - OVMAX + np.arange(width)
        near = start - HALO + np.arange(block + 2 * HALO)

        def pick(rows, cols):
            good = ((rows >= 0) & (rows < ctrl))[:, None] & ((cols >= 0) & (cols < ctrl))[None, :]
            return np.where(good, gram[np.clip(rows, 0, ctrl - 1)][:, np.clip(cols, 0, ctrl - 1)], 0.0)

        full, rows = pick(knots, knots), pick(knots, near)
        for low in range(OVMAX + 1):
            for up in range(OVMAX + 1):
                weight = (knots >= start - low) & (knots < start + block + up) & (knots >= 0) & (knots < ctrl)
                weight = weight.astype(np.float64)
                local = full * weight[:, None] * weight[None, :] + np.diag(1.0 - weight)
                own = (np.linalg.inv(local) * weight[None, :])[OVMAX : OVMAX + block]
                out[kind, low, up, 0, :, :width] = own
                out[kind, low, up, 1] = own @ rows
    return out.reshape(-1, 2 * block, block + 2 * HALO).astype(np.float32)


def kernel(
    nx, ny, cx, cy, nz, chunks,
    margin, field, kappa, velo, zmat_h, ymat_h, tab_h,
    adv, ctrl_out,
    U, kb, vb, kk, ky, kz, hx, hy, hz, hzp, ys, yr, gy, kxr, hxr,
    xps, xpr, xc, zf, a2s, a2r, bs, rh, ce, zmat, ymat, tab,
    in_sem, cst_sem, xs_sem, xr_sem, ki_s, ki_r, ys_sem, yr_sem, ps_sem, pr_sem,
    as_sem, ar_sem, bs_sem, br_sem, hs_sem, hr_sem, cs_sem, cr_sem,
):
    px, py = lax.axis_index("px"), lax.axis_index("py")
    rows = cx // chunks
    block = cx // 2
    mine = block // ny
    own = cy // 2
    zc = nz // 2

    loads = [
        pltpu.make_async_copy(kappa, kb, in_sem.at[0]),
        pltpu.make_async_copy(velo, vb, in_sem.at[1]),
        pltpu.make_async_copy(field, U.at[0, pl.ds(1, cx)], in_sem.at[2]),
    ]
    consts = [
        pltpu.make_async_copy(zmat_h, zmat, cst_sem.at[0]),
        pltpu.make_async_copy(ymat_h, ymat, cst_sem.at[1]),
        pltpu.make_async_copy(tab_h, tab, cst_sem.at[2]),
    ]
    for c in loads + consts:
        c.start()

    zero_face = jnp.zeros((cy, nz), jnp.float32)
    for s in range(2):
        U[s, 0] = zero_face
        U[s, cx + 1] = zero_face
        kxr[s] = jnp.zeros((cy, nz), kxr.dtype)
        hxr[s] = jnp.zeros((cy, nz), hxr.dtype)
        xpr[s] = jnp.zeros((2, cy, nz), jnp.float32)
    yr[...] = jnp.zeros(yr.shape, jnp.float32)
    rh[...] = jnp.zeros(rh.shape, jnp.float32)
    ce[0:HALO] = jnp.zeros((HALO, own * zc), jnp.float32)
    ce[HALO + block :] = jnp.zeros((HALO, own * zc), jnp.float32)
    zf[...] = jnp.zeros(zf.shape, jnp.float32)

    barrier = pltpu.get_barrier_semaphore()

    @pl.loop(1, ny)
    def _(d):
        pl.semaphore_signal(barrier, inc=1, device_id=(px, lax.rem(py + d, ny)), device_id_type=MESH)

    has = {0: px > 0, 1: px < nx - 1}
    to = {0: (px - 1, py), 1: (px + 1, py)}
    hasy = {0: py > 0, 1: py < ny - 1}
    toy = {0: (px, py - 1), 1: (px, py + 1)}
    for side in (0, 1):

        @pl.when(has[side])
        def _(side=side):
            pl.semaphore_signal(barrier, inc=1, device_id=to[side], device_id_type=MESH)

    neighbours = jnp.where(px > 0, 1, 0) + jnp.where(px < nx - 1, 1, 0)
    pl.semaphore_wait(barrier, ny - 1 + neighbours)

    def remote(src, dst, ss, rs, dev):
        return pltpu.make_async_remote_copy(
            src_ref=src, dst_ref=dst, send_sem=ss, recv_sem=rs, device_id=dev, device_id_type=MESH
        )

    def x_init(side):
        edge = 0 if side == 0 else cx - 1
        return [
            remote(kappa.at[edge], kxr.at[1 - side], ki_s.at[0, side], ki_r.at[0, 1 - side], to[side]),
            remote(velo.at[0, edge], hxr.at[1 - side], ki_s.at[1, side], ki_r.at[1, 1 - side], to[side]),
            remote(
                field.at[edge],
                U.at[0, cx + 1 if side == 0 else 0],
                xs_sem.at[0, side],
                xr_sem.at[0, 1 - side],
                to[side],
            ),
        ]

    def x_face(t, side):
        slot = t % 2
        return remote(
            U.at[slot, 1 if side == 0 else cx],
            U.at[slot, cx + 1 if side == 0 else 0],
            xs_sem.at[t, side],
            xr_sem.at[t, 1 - side],
            to[side],
        )

    def y_face(t, c, side):
        items = pl.ds(0, 3) if t == 0 else pl.ds(t + 2, 1)
        part = pl.ds(c * rows, rows)
        return remote(
            ys.at[side, items, part],
            yr.at[1 - side, items, part],
            ys_sem.at[t, c, side],
            yr_sem.at[t, c, 1 - side],
            toy[side],
        )

    def y_arrival(t, c, side):
        items = pl.ds(0, 3) if t == 0 else pl.ds(t + 2, 1)
        part = pl.ds(c * rows, rows)
        return remote(
            ys.at[side, items, part],
            yr.at[side, items, part],
            ys_sem.at[t, c, side],
            yr_sem.at[t, c, side],
            toy[side],
        )

    def x_arrival(t, side):
        slot = t % 2
        return remote(
            U.at[slot, 1],
            U.at[slot, 0 if side == 0 else cx + 1],
            xs_sem.at[t, side],
            xr_sem.at[t, side],
            to[side],
        )

    def when_do(cond, do):
        pl.when(cond)(do)

    for side in (0, 1):

        @pl.when(has[side])
        def _(side=side):
            for c in x_init(side):
                c.start()

    for c in loads:
        c.wait()

    lane = lax.broadcasted_iota(jnp.int32, (cy, nz), 1)
    row = lax.broadcasted_iota(jnp.int32, (cy, nz), 0)
    last_lane, first_lane = lane == nz - 1, lane == 0
    last_row, first_row = row == cy - 1, row == 0

    def prepare(x):
        k = kb[x].astype(jnp.float32) * 0.05
        kk[x + 1] = k
        ky[x] = k + pltpu.roll(k, cy - 1, 0)
        kz[x] = k + jnp.where(last_lane, 0.0, pltpu.roll(k, nz - 1, 1))
        hx[x + 1] = vb[0, x].astype(jnp.float32) * 0.025
        h = vb[1, x].astype(jnp.float32) * 0.025
        hy[x] = h
        g = vb[2, x].astype(jnp.float32) * 0.025
        hz[x] = g
        hzp[x] = jnp.where(last_lane, 0.0, pltpu.roll(g, nz - 1, 1))
        u = U[0, x + 1]
        at = pl.ds(x, 1)
        for side, pick in ((0, slice(0, 1)), (1, slice(cy - 1, cy))):
            ys[side, 0, at] = k[pick]
            ys[side, 1, at] = h[pick]
            ys[side, 2, at] = u[pick]

    for c in range(chunks):

        @pl.loop(0, rows)
        def _(i, c=c):
            prepare(c * rows + i)

        for side in (0, 1):
            when_do(hasy[side], lambda c=c, side=side: y_face(0, c, side).start())

    for side in (0, 1):

        @pl.when(has[side])
        def _(side=side):
            remote(kappa.at[0], kxr.at[side], ki_s.at[0, side], ki_r.at[0, side], to[side]).wait_recv()
            remote(velo.at[0, 0], hxr.at[side], ki_s.at[1, side], ki_r.at[1, side], to[side]).wait_recv()

        at = 0 if side == 0 else cx + 1
        kk[at] = kxr[side].astype(jnp.float32) * 0.05
        hx[at] = hxr[side].astype(jnp.float32) * 0.025

    def x_flux(s, x):
        u, up = U[s, x], U[s, x + 1]
        return (kk[x] + kk[x + 1]) * (up - u) - (hx[x] * (u * u) + hx[x + 1] * (up * up))

    def partial(side):
        for q in range(2):
            k = (q - 2) if side == 0 else block + q
            total = None
            for j in range(8):
                i = 2 * k - 3 + j
                if 0 <= i < cx:
                    term = TAPS[j] * adv[i]
                    total = term if total is None else total + term
            xps[side, q] = total
        return remote(xps.at[side], xpr.at[1 - side], ps_sem.at[side], pr_sem.at[1 - side], to[side])

    order = [0, chunks - 1] + list(range(1, chunks - 1)) if chunks > 1 else [0]
    for t in range(STEPS):
        s = t % 2
        last = t == STEPS - 1
        for c in order:
            if c == 0:
                when_do(has[0], lambda t=t: x_arrival(t, 0).wait_recv())
            if c == chunks - 1:
                when_do(has[1], lambda t=t: x_arrival(t, 1).wait_recv())
            for side in (0, 1):
                when_do(hasy[side], lambda t=t, c=c, side=side: y_arrival(t, c, side).wait_recv())
            part = pl.ds(c * rows, rows)
            for side in (0, 1):
                a, b = ys[side, t + 2, part], yr[side, t + 2, part]
                diff = (a - b) if side == 0 else (b - a)
                gy[side, part] = (ys[side, 0, part] + yr[side, 0, part]) * diff - (
                    ys[side, 1, part] * (a * a) + yr[side, 1, part] * (b * b)
                )

            def line(i, flux, t=t, s=s, c=c, last=last):
                x = c * rows + i
                u, k = U[s, x + 1], kk[x + 1]
                up = U[s, x + 2]
                sq = u * u
                gx = (k + kk[x + 2]) * (up - u) - (hx[x + 1] * sq + hx[x + 2] * (up * up))
                fy = hy[x] * sq
                g = ky[x] * (pltpu.roll(u, cy - 1, 0) - u) - (fy + pltpu.roll(fy, cy - 1, 0))
                at = pl.ds(x, 1)
                g = jnp.where(last_row, gy[1, at], g)
                gym = jnp.where(first_row, gy[0, at], pltpu.roll(g, 1, 0))
                uz = jnp.where(last_lane, 0.0, pltpu.roll(u, nz - 1, 1))
                fz = hz[x] * sq
                gz = kz[x] * (uz - u) - (fz + hzp[x] * (uz * uz))
                gzm = jnp.where(first_lane, k * u - fz, pltpu.roll(gz, 1, 1))
                new = u + ((gx - flux) + (g - gym) + (gz - gzm))
                if last:
                    adv[x] = new
                else:
                    U[1 - s, x + 1] = new
                    ys[0, t + 3, at] = new[0:1]
                    ys[1, t + 3, at] = new[cy - 1 : cy]
                return gx

            lax.fori_loop(0, rows, line, x_flux(s, c * rows))
            if not last:
                for side in (0, 1):
                    when_do(hasy[side], lambda t=t, c=c, side=side: y_face(t + 1, c, side).start())
                if c == 0:
                    when_do(has[0], lambda t=t: x_face(t + 1, 0).start())
                if c == chunks - 1:
                    when_do(has[1], lambda t=t: x_face(t + 1, 1).start())
            else:
                for side, at in ((0, 0), (1, chunks - 1)):
                    if c == at:
                        copy = partial(side)
                        when_do(has[side], lambda copy=copy: copy.start())
        for side in (0, 1):

            @pl.when(has[side])
            def _(t=t, side=side):
                x_face(t, side).wait_send()
                if t == 0:
                    for c in x_init(side)[:2]:
                        c.wait_send()

            @pl.when(hasy[side])
            def _(t=t, side=side):
                for c in range(chunks):
                    y_face(t, c, side).wait_send()

    def x_row(k, low, high):
        total = None
        for j in range(8):
            if low <= j < high:
                term = TAPS[j] * adv[2 * k - 3 + j]
                total = term if total is None else total + term
        return total

    for k in (0, 1):
        xc[k] = x_row(k, 3 - 2 * k, 8)
    for k in (block - 2, block - 1):
        xc[k] = x_row(k, 0, cx - 2 * k + 3)

    @pl.loop(2, block - 2)
    def _(k):
        xc[k] = x_row(k, 0, 8)

    for side in (0, 1):

        @pl.when(has[side])
        def _(side=side):
            c = remote(xps.at[side], xpr.at[side], ps_sem.at[side], pr_sem.at[side], to[side])
            c.wait()

        for q in range(2):
            k = q if side == 0 else block - 2 + q
            xc[k] += xpr[side, q]

    for c in consts:
        c.wait()

    def group(peer):
        first = peer * mine
        lines = xc[pl.ds(first, mine)].reshape(mine * cy, nz)
        fitted = jnp.dot(lines, zmat[...], precision=HIGH, preferred_element_type=jnp.float32)
        zf[:, 8 : 8 + cy, :] = fitted.reshape(mine, cy, zc)
        for a in range(mine):
            total = None
            for j in range(8):
                term = TAPS[j] * zf[a, pl.ds(1 + j, QROWS, stride=2), :]
                total = term if total is None else total + term
            a2s[peer, a] = total

    def a2a(peer):
        return remote(a2s.at[peer], a2r.at[py], as_sem.at[peer], ar_sem.at[py], (px, peer))

    @pl.loop(1, ny)
    def _(d):
        peer = lax.rem(py + d, ny)
        group(peer)
        a2a(peer).start()

    group(py)
    a2r[py] = a2s[py]

    @pl.loop(1, ny)
    def _(d):
        peer = lax.rem(py + d, ny)
        remote(a2s.at[peer], a2r.at[peer], as_sem.at[peer], ar_sem.at[peer], (px, peer)).wait()

    gathered = jnp.concatenate([a2r[:, a].reshape(ny * QROWS, zc) for a in range(mine)], axis=1)
    solved = jnp.dot(ymat[...], gathered, precision=HIGH, preferred_element_type=jnp.float32)
    for q in range(ny):
        for a in range(mine):
            bs[q, a * own : (a + 1) * own] = solved[q * own : (q + 1) * own, a * zc : (a + 1) * zc]

    span = mine * own
    base = OVMAX * own

    def back(peer):
        return remote(
            bs.at[peer], rh.at[pl.ds(base + py * span, span)], bs_sem.at[peer], br_sem.at[py], (px, peer)
        )

    @pl.loop(1, ny)
    def _(d):
        back(lax.rem(py + d, ny)).start()

    rh[pl.ds(base + py * span, span)] = bs[py]

    @pl.loop(1, ny)
    def _(d):
        peer = lax.rem(py + d, ny)
        remote(
            bs.at[peer], rh.at[pl.ds(base + peer * span, span)], bs_sem.at[peer], br_sem.at[peer], (px, peer)
        ).wait()

    def margin_copy(side):
        size = OVMAX * own
        src = base if side == 0 else block * own
        dst = base + block * own if side == 0 else 0
        return remote(
            rh.at[pl.ds(src, size)], rh.at[pl.ds(dst, size)], hs_sem.at[side], hr_sem.at[1 - side], to[side]
        )

    def control_copy(side):
        src = HALO if side == 0 else block
        dst = HALO + block if side == 0 else 0
        return remote(
            ce.at[pl.ds(src, HALO)], ce.at[pl.ds(dst, HALO)], cs_sem.at[side], cr_sem.at[1 - side], to[side]
        )

    def exchange(make, arrive):
        for side in (0, 1):
            when_do(has[side], lambda side=side: make(side).start())
        for side in (0, 1):

            @pl.when(has[side])
            def _(side=side):
                make(side).wait_send()
                arrive(side).wait_recv()

    size = OVMAX * own
    exchange(
        margin_copy,
        lambda side: remote(
            rh.at[pl.ds(base, size)],
            rh.at[pl.ds(0 if side == 0 else base + block * own, size)],
            hs_sem.at[side],
            hr_sem.at[side],
            to[side],
        ),
    )
    kind = jnp.where(px == 0, 0, jnp.where(px == nx - 1, 2, 1))
    index = (kind * (OVMAX + 1) + margin[0, 0]) * (OVMAX + 1) + margin[0, 1]
    mats = tab[index]
    width = block + 2 * OVMAX
    right = jnp.concatenate([rh[pl.ds(m, width, stride=own), :] for m in range(own)], axis=1)
    first = jnp.dot(mats[:block, :width], right, precision=HIGH, preferred_element_type=jnp.float32)
    ce[HALO : HALO + block] = first
    exchange(
        control_copy,
        lambda side: remote(
            ce.at[pl.ds(HALO, HALO)],
            ce.at[pl.ds(0 if side == 0 else HALO + block, HALO)],
            cs_sem.at[side],
            cr_sem.at[side],
            to[side],
        ),
    )
    second = jnp.dot(mats[block:], ce[...], precision=HIGH, preferred_element_type=jnp.float32)
    final = 2.0 * first - second
    for m in range(own):
        ctrl_out[pl.ds(m, block, stride=own), :] = final[:, m * zc : (m + 1) * zc]


def per_device(field, diffusivity, velocity, margin):
    cx, cy, nz = field.shape
    nx, ny = lax.axis_size("px"), lax.axis_size("py")
    chunks = 4
    block, own, zc = cx // 2, cy // 2, nz // 2
    mine = block // ny
    zmat = jnp.asarray(z_matrix(nz))
    ymat = jnp.asarray(y_matrix(cy * ny, ny))
    tab = jnp.asarray(schwarz_table(cx * nx, nx))
    f32, bf16 = jnp.float32, jnp.bfloat16
    V, D = pltpu.VMEM, pltpu.SemaphoreType.DMA
    slab = (cx, cy, nz)
    scratch = [
        V((2, cx + 2, cy, nz), f32),
        V(slab, bf16),
        V((3,) + slab, bf16),
        V((cx + 2, cy, nz), f32),
        V(slab, f32),
        V(slab, f32),
        V((cx + 2, cy, nz), f32),
        V(slab, f32),
        V(slab, f32),
        V(slab, f32),
        V((2, STEPS + 2, cx, nz), f32),
        V((2, STEPS + 2, cx, nz), f32),
        V((2, cx, nz), f32),
        V((2, cy, nz), bf16),
        V((2, cy, nz), bf16),
        V((2, 2, cy, nz), f32),
        V((2, 2, cy, nz), f32),
        V((block, cy, nz), f32),
        V((mine, cy + 24, zc), f32),
        V((ny, mine, QROWS, zc), f32),
        V((ny, mine, QROWS, zc), f32),
        V((ny, mine * own, zc), f32),
        V(((block + 2 * OVMAX) * own, zc), f32),
        V((block + 2 * HALO, own * zc), f32),
        V(zmat.shape, f32),
        V(ymat.shape, f32),
        V(tab.shape, f32),
        D((3,)),
        D((3,)),
        D((STEPS, 2)),
        D((STEPS, 2)),
        D((2, 2)),
        D((2, 2)),
        D((STEPS, chunks, 2)),
        D((STEPS, chunks, 2)),
        D((2,)),
        D((2,)),
        D((ny,)),
        D((ny,)),
        D((ny,)),
        D((ny,)),
        D((2,)),
        D((2,)),
        D((2,)),
        D((2,)),
    ]
    hbm = pl.BlockSpec(memory_space=pl.ANY)
    vmem = pl.BlockSpec(memory_space=pltpu.VMEM)
    adv, ctrl = pl.pallas_call(
        functools.partial(kernel, nx, ny, cx, cy, nz, chunks),
        out_shape=(
            jax.ShapeDtypeStruct(slab, f32),
            jax.ShapeDtypeStruct((block * own, zc), f32),
        ),
        in_specs=[pl.BlockSpec(memory_space=pltpu.SMEM)] + [hbm] * 6,
        out_specs=(vmem, vmem),
        scratch_shapes=scratch,
        compiler_params=pltpu.CompilerParams(
            collective_id=0, has_side_effects=True, vmem_limit_bytes=60 * 2**20
        ),
    )(margin, field, diffusivity, velocity, zmat, ymat, tab)
    return adv, ctrl.reshape(block, own, zc)


def solution(mesh):
    placed = (P("px", "py", None), P("px", "py", None), P(None, "px", "py", None), P("px", None))
    return jax.shard_map(
        per_device,
        mesh=mesh,
        in_specs=placed,
        out_specs=(P("px", "py", None), P("px", "py", None)),
        check_vma=False,
    )
```

```python
import functools

import jax
import jax.numpy as jnp
import numpy as np
from jax import lax
from jax.experimental import pallas as pl
from jax.experimental.pallas import tpu as pltpu
from jax.sharding import PartitionSpec as P

STEPS = 4
OVMAX = 4
HALO = 8
QROWS = 24
UNROLL = 4
MESH = pl.DeviceIdType.MESH


def bspline(t):
    t = np.abs(t)
    inner = (4.0 - 6.0 * t * t + 3.0 * t**3) / 6.0
    outer = np.maximum(2.0 - t, 0.0) ** 3 / 6.0
    return np.where(t < 1.0, inner, outer)


def basis(total):
    j = np.arange(total, dtype=np.float64)[:, None]
    k = np.arange(total // 2, dtype=np.float64)[None, :]
    return bspline(0.5 * (j - 2.0 * k - 0.5))


TAPS = [float(bspline(0.5 * (j - 3.5))) for j in range(8)]


def z_matrix(total):
    table = basis(total)
    return np.linalg.solve(table.T @ table, table.T).T.astype(np.float32)


def y_matrix(total, count):
    table = basis(total)
    inverse = np.linalg.inv(table.T @ table)
    ctrl = total // 2
    own = ctrl // count
    result = np.zeros((ctrl, count, QROWS))
    for p in range(count):
        for q in range(own + 4):
            k = own * p - 2 + q
            if 0 <= k < ctrl:
                result[:, p, q] = inverse[:, k]
    return result.reshape(ctrl, count * QROWS).astype(np.float32)


def schwarz_table(total, count):
    table = basis(total)
    gram = table.T @ table
    ctrl = total // 2
    block = ctrl // count
    width = block + 2 * OVMAX
    out = np.zeros((3, OVMAX + 1, OVMAX + 1, 2, block, block + 2 * HALO))
    for kind, p in enumerate((0, min(1, count - 1), count - 1)):
        start = p * block
        knots = start - OVMAX + np.arange(width)
        near = start - HALO + np.arange(block + 2 * HALO)

        def pick(rows, cols):
            good = ((rows >= 0) & (rows < ctrl))[:, None] & ((cols >= 0) & (cols < ctrl))[None, :]
            return np.where(good, gram[np.clip(rows, 0, ctrl - 1)][:, np.clip(cols, 0, ctrl - 1)], 0.0)

        full, rows = pick(knots, knots), pick(knots, near)
        for low in range(OVMAX + 1):
            for up in range(OVMAX + 1):
                weight = (knots >= start - low) & (knots < start + block + up) & (knots >= 0) & (knots < ctrl)
                weight = weight.astype(np.float64)
                local = full * weight[:, None] * weight[None, :] + np.diag(1.0 - weight)
                own = (np.linalg.inv(local) * weight[None, :])[OVMAX : OVMAX + block]
                out[kind, low, up, 0, :, :width] = own
                out[kind, low, up, 1] = own @ rows
    return out.reshape(-1, 2 * block, block + 2 * HALO).astype(np.float32)


def split(a):
    top = a.astype(jnp.bfloat16)
    return top, (a - top.astype(jnp.float32)).astype(jnp.bfloat16)


def product(a, b):
    dot = functools.partial(jnp.dot, preferred_element_type=jnp.float32)
    return dot(a[0], b[0]) + (dot(a[0], b[1]) + dot(a[1], b[0]))


def halves(a):
    top = a.astype(jnp.bfloat16)
    return jnp.asarray(np.stack([top, (a - top.astype(np.float32)).astype(jnp.bfloat16)]))


def kernel(
    nx, ny, cx, cy, nz, chunks,
    margin, field, kappa, velo, zmat_h, ymat_h, tab_h,
    adv, ctrl_out,
    U, kb, vb, kk, ky, kz, hx, hy, hz, ys, yr, gy, kxr, hxr,
    xps, xpr, xc, zf, a2s, a2r, bs, rh, ce, zmat, ymat, tab,
    in_sem, cst_sem, xs_sem, xr_sem, ki_s, ki_r, ys_sem, yr_sem, ps_sem, pr_sem,
    as_sem, ar_sem, bs_sem, br_sem, hs_sem, hr_sem, cs_sem, cr_sem,
):
    px, py = lax.axis_index("px"), lax.axis_index("py")
    rows = cx // chunks
    block = cx // 2
    mine = block // ny
    own = cy // 2
    zc = nz // 2

    loads = [
        pltpu.make_async_copy(kappa, kb, in_sem.at[0]),
        pltpu.make_async_copy(velo, vb, in_sem.at[1]),
        pltpu.make_async_copy(field, U.at[0, pl.ds(1, cx)], in_sem.at[2]),
    ]
    consts = [
        pltpu.make_async_copy(zmat_h, zmat, cst_sem.at[0]),
        pltpu.make_async_copy(ymat_h, ymat, cst_sem.at[1]),
        pltpu.make_async_copy(tab_h, tab, cst_sem.at[2]),
    ]
    for c in loads + consts:
        c.start()

    zero_face = jnp.zeros((cy, nz), jnp.float32)
    for s in range(2):
        U[s, 0] = zero_face
        U[s, cx + 1] = zero_face
        kxr[s] = jnp.zeros((cy, nz), kxr.dtype)
        hxr[s] = jnp.zeros((cy, nz), hxr.dtype)
        xpr[s] = jnp.zeros((2, cy, nz), jnp.float32)
    yr[...] = jnp.zeros(yr.shape, jnp.float32)
    rh[...] = jnp.zeros(rh.shape, jnp.float32)
    ce[0:HALO] = jnp.zeros((HALO, own * zc), jnp.float32)
    ce[HALO + block :] = jnp.zeros((HALO, own * zc), jnp.float32)
    zf[...] = jnp.zeros(zf.shape, jnp.float32)
    a2r[...] = jnp.zeros(a2r.shape, jnp.float32)

    barrier = pltpu.get_barrier_semaphore()

    @pl.loop(1, ny)
    def _(d):
        pl.semaphore_signal(barrier, inc=1, device_id=(px, lax.rem(py + d, ny)), device_id_type=MESH)

    has = {0: px > 0, 1: px < nx - 1}
    to = {0: (px - 1, py), 1: (px + 1, py)}
    hasy = {0: py > 0, 1: py < ny - 1}
    toy = {0: (px, py - 1), 1: (px, py + 1)}
    for side in (0, 1):

        @pl.when(has[side])
        def _(side=side):
            pl.semaphore_signal(barrier, inc=1, device_id=to[side], device_id_type=MESH)

    neighbours = jnp.where(px > 0, 1, 0) + jnp.where(px < nx - 1, 1, 0)
    pl.semaphore_wait(barrier, ny - 1 + neighbours)

    def remote(src, dst, ss, rs, dev):
        return pltpu.make_async_remote_copy(
            src_ref=src, dst_ref=dst, send_sem=ss, recv_sem=rs, device_id=dev, device_id_type=MESH
        )

    def x_init(side):
        edge = 0 if side == 0 else cx - 1
        return [
            remote(kappa.at[edge], kxr.at[1 - side], ki_s.at[0, side], ki_r.at[0, 1 - side], to[side]),
            remote(velo.at[0, edge], hxr.at[1 - side], ki_s.at[1, side], ki_r.at[1, 1 - side], to[side]),
            remote(
                field.at[edge],
                U.at[0, cx + 1 if side == 0 else 0],
                xs_sem.at[0, side],
                xr_sem.at[0, 1 - side],
                to[side],
            ),
        ]

    def x_face(t, side):
        slot = t % 2
        return remote(
            U.at[slot, 1 if side == 0 else cx],
            U.at[slot, cx + 1 if side == 0 else 0],
            xs_sem.at[t, side],
            xr_sem.at[t, 1 - side],
            to[side],
        )

    def y_face(t, c, side):
        items = pl.ds(0, 3) if t == 0 else pl.ds(t + 2, 1)
        part = pl.ds(c * rows, rows)
        return remote(
            ys.at[side, items, part],
            yr.at[1 - side, items, part],
            ys_sem.at[t, c, side],
            yr_sem.at[t, c, 1 - side],
            toy[side],
        )

    def y_arrival(t, c, side):
        items = pl.ds(0, 3) if t == 0 else pl.ds(t + 2, 1)
        part = pl.ds(c * rows, rows)
        return remote(
            ys.at[side, items, part],
            yr.at[side, items, part],
            ys_sem.at[t, c, side],
            yr_sem.at[t, c, side],
            toy[side],
        )

    def x_arrival(t, side):
        slot = t % 2
        return remote(
            U.at[slot, 1],
            U.at[slot, 0 if side == 0 else cx + 1],
            xs_sem.at[t, side],
            xr_sem.at[t, side],
            to[side],
        )

    def when_do(cond, do):
        pl.when(cond)(do)

    for side in (0, 1):

        @pl.when(has[side])
        def _(side=side):
            for c in x_init(side):
                c.start()

    for c in loads:
        c.wait()

    lane = lax.broadcasted_iota(jnp.int32, (cy, nz), 1)
    last_lane = lane == nz - 1

    def prepare(x):
        k = kb[x].astype(jnp.float32) * 0.05
        kk[x + 1] = k
        ky[x] = k + pltpu.roll(k, cy - 1, 0)
        kz[x] = k + jnp.where(last_lane, 0.0, pltpu.roll(k, nz - 1, 1))
        hx[x + 1] = vb[0, x].astype(jnp.float32) * 0.025
        h = vb[1, x].astype(jnp.float32) * 0.025
        hy[x] = h
        g = vb[2, x].astype(jnp.float32) * 0.025
        hz[x] = g
        u = U[0, x + 1]
        at = pl.ds(x, 1)
        for side, pick in ((0, slice(0, 1)), (1, slice(cy - 1, cy))):
            ys[side, 0, at] = k[pick]
            ys[side, 1, at] = h[pick]
            ys[side, 2, at] = u[pick]

    for c in range(chunks):

        @pl.loop(0, rows)
        def _(i, c=c):
            prepare(c * rows + i)

        for side in (0, 1):
            when_do(hasy[side], lambda c=c, side=side: y_face(0, c, side).start())

    for side in (0, 1):

        @pl.when(has[side])
        def _(side=side):
            remote(kappa.at[0], kxr.at[side], ki_s.at[0, side], ki_r.at[0, side], to[side]).wait_recv()
            remote(velo.at[0, 0], hxr.at[side], ki_s.at[1, side], ki_r.at[1, side], to[side]).wait_recv()

        at = 0 if side == 0 else cx + 1
        kk[at] = kxr[side].astype(jnp.float32) * 0.05
        hx[at] = hxr[side].astype(jnp.float32) * 0.025

    tiles = [(slice(8 * i, 8 * i + 8), slice(128 * j, 128 * j + 128)) for i in range(cy // 8) for j in range(nz // 128)]
    high, wide = cy // 8, nz // 128
    trow = lax.broadcasted_iota(jnp.int32, (8, 128), 0)
    tlane = lax.broadcasted_iota(jnp.int32, (8, 128), 1)
    row_end, row_start = trow == 7, trow == 0
    lane_end, lane_start = tlane == 127, tlane == 0

    def x_start(s, x):
        flux, force = [], []
        for a, b in tiles:
            u, up = U[s, x, a, b], U[s, x + 1, a, b]
            fp = hx[x + 1, a, b] * (up * up)
            flux.append((kk[x, a, b] + kk[x + 1, a, b]) * (up - u) - (hx[x, a, b] * (u * u) + fp))
            force.append(fp)
        return tuple(flux), tuple(force)

    def partial(side):
        for q in range(2):
            k = (q - 2) if side == 0 else block + q
            total = None
            for j in range(8):
                i = 2 * k - 3 + j
                if 0 <= i < cx:
                    term = TAPS[j] * adv[i]
                    total = term if total is None else total + term
            xps[side, q] = total
        return remote(xps.at[side], xpr.at[1 - side], ps_sem.at[side], pr_sem.at[1 - side], to[side])

    order = [0, chunks - 1] + list(range(1, chunks - 1)) if chunks > 1 else [0]
    for t in range(STEPS):
        s = t % 2
        last = t == STEPS - 1
        for c in order:
            if c == 0:
                when_do(has[0], lambda t=t: x_arrival(t, 0).wait_recv())
            if c == chunks - 1:
                when_do(has[1], lambda t=t: x_arrival(t, 1).wait_recv())
            for side in (0, 1):
                when_do(hasy[side], lambda t=t, c=c, side=side: y_arrival(t, c, side).wait_recv())
            part = pl.ds(c * rows, rows)
            for side in (0, 1):
                a, b = ys[side, t + 2, part], yr[side, t + 2, part]
                diff = (a - b) if side == 0 else (b - a)
                gy[side, part] = (ys[side, 0, part] + yr[side, 0, part]) * diff - (
                    ys[side, 1, part] * (a * a) + yr[side, 1, part] * (b * b)
                )

            def line(x, carry, s=s):
                flux, force = carry
                at = pl.ds(x, 1)
                n = len(tiles)
                low_face, top_face = gy[0, at], gy[1, at]
                u = [U[s, x + 1, a, b] for a, b in tiles]
                sq = [v * v for v in u]
                gx, fx, new = [], [], []
                for m, (a, b) in enumerate(tiles):
                    up = U[s, x + 2, a, b]
                    fp = hx[x + 2, a, b] * (up * up)
                    g = (kk[x + 1, a, b] + kk[x + 2, a, b]) * (up - u[m]) - (force[m] + fp)
                    gx.append(g)
                    fx.append(fp)
                    new.append(u[m] + (g - flux[m]))
                ru = [pltpu.roll(v, 7, 0) for v in u]
                fy = [hy[x, a, b] * sq[m] for m, (a, b) in enumerate(tiles)]
                rf = [pltpu.roll(v, 7, 0) for v in fy]
                before = [None] * wide
                for m, (a, b) in enumerate(tiles):
                    j = m % wide
                    if m + wide < n:
                        up = jnp.where(row_end, ru[m + wide], ru[m])
                        fp = jnp.where(row_end, rf[m + wide], rf[m])
                    else:
                        up, fp = ru[m], rf[m]
                    g = ky[x, a, b] * (up - u[m]) - (fy[m] + fp)
                    if m + wide >= n:
                        g = jnp.where(row_end, top_face[:, b], g)
                    rg = pltpu.roll(g, 1, 0)
                    low = low_face[:, b] if m < wide else before[j]
                    new[m] = new[m] + (g - jnp.where(row_start, low, rg))
                    before[j] = rg
                for r in range(high):
                    fz = [hz[x, a, b] * sq[r * wide + j] for j, (a, b) in enumerate(tiles[r * wide : r * wide + wide])]
                    ru = [pltpu.roll(u[r * wide + j], 127, 1) for j in range(wide)]
                    rf = [pltpu.roll(v, 127, 1) for v in fz]
                    prev = None
                    for j in range(wide):
                        m = r * wide + j
                        a, b = tiles[m]
                        up = jnp.where(lane_end, ru[j + 1] if j + 1 < wide else 0.0, ru[j])
                        fp = jnp.where(lane_end, rf[j + 1] if j + 1 < wide else 0.0, rf[j])
                        g = kz[x, a, b] * (up - u[m]) - (fz[j] + fp)
                        rg = pltpu.roll(g, 1, 1)
                        low = kk[x + 1, a, b] * u[m] - fz[j] if j == 0 else prev
                        new[m] = new[m] + (g - jnp.where(lane_start, low, rg))
                        prev = rg
                return new, (tuple(gx), tuple(fx))

            def lines(i, carry, t=t, s=s, c=c, last=last):
                fresh = []
                for r in range(UNROLL):
                    x = c * rows + UNROLL * i + r
                    new, carry = line(x, carry)
                    fresh.append((x, new))
                for x, new in fresh:
                    at = pl.ds(x, 1)
                    for m, (a, b) in enumerate(tiles):
                        if last:
                            adv[x, a, b] = new[m]
                        else:
                            U[1 - s, x + 1, a, b] = new[m]
                    if not last:
                        ys[0, t + 3, at] = jnp.concatenate([v[0:1] for v in new[:wide]], axis=1)
                        ys[1, t + 3, at] = jnp.concatenate([v[7:8] for v in new[-wide:]], axis=1)
                return carry

            lax.fori_loop(0, rows // UNROLL, lines, x_start(s, c * rows))
            if not last:
                for side in (0, 1):
                    when_do(hasy[side], lambda t=t, c=c, side=side: y_face(t + 1, c, side).start())
                if c == 0:
                    when_do(has[0], lambda t=t: x_face(t + 1, 0).start())
                if c == chunks - 1:
                    when_do(has[1], lambda t=t: x_face(t + 1, 1).start())
            else:
                for side, at in ((0, 0), (1, chunks - 1)):
                    if c == at:
                        copy = partial(side)
                        when_do(has[side], lambda copy=copy: copy.start())
        for side in (0, 1):

            @pl.when(has[side])
            def _(t=t, side=side):
                x_face(t, side).wait_send()
                if t == 0:
                    for c in x_init(side)[:2]:
                        c.wait_send()

            @pl.when(hasy[side])
            def _(t=t, side=side):
                for c in range(chunks):
                    y_face(t, c, side).wait_send()

    def x_row(k, low, high):
        total = None
        for j in range(8):
            if low <= j < high:
                term = TAPS[j] * adv[2 * k - 3 + j]
                total = term if total is None else total + term
        return total

    for k in (0, 1):
        xc[k] = x_row(k, 3 - 2 * k, 8)
    for k in (block - 2, block - 1):
        xc[k] = x_row(k, 0, cx - 2 * k + 3)

    @pl.loop(2, block - 2)
    def _(k):
        xc[k] = x_row(k, 0, 8)

    for side in (0, 1):

        @pl.when(has[side])
        def _(side=side):
            c = remote(xps.at[side], xpr.at[side], ps_sem.at[side], pr_sem.at[side], to[side])
            c.wait()

        for q in range(2):
            k = q if side == 0 else block - 2 + q
            xc[k] += xpr[side, q]

    for c in consts:
        c.wait()

    def group(peer):
        first = peer * mine
        lines = xc[pl.ds(first, mine)].reshape(mine * cy, nz)
        fitted = product(split(lines), (zmat[0], zmat[1]))
        zf[:, 8 : 8 + cy, :] = fitted.reshape(mine, cy, zc)
        for a in range(mine):
            total = None
            for j in range(8):
                term = TAPS[j] * zf[a, pl.ds(1 + j, QROWS, stride=2), :]
                total = term if total is None else total + term
            a2s[peer, a] = total

    used = pl.ds(0, own + 4)

    def a2a(peer):
        return remote(a2s.at[peer, :, used], a2r.at[py, :, used], as_sem.at[peer], ar_sem.at[py], (px, peer))

    @pl.loop(1, ny)
    def _(d):
        peer = lax.rem(py + d, ny)
        group(peer)
        a2a(peer).start()

    group(py)
    a2r[py] = a2s[py]

    @pl.loop(1, ny)
    def _(d):
        peer = lax.rem(py + d, ny)
        remote(a2s.at[peer, :, used], a2r.at[peer, :, used], as_sem.at[peer], ar_sem.at[peer], (px, peer)).wait()

    gathered = jnp.concatenate([a2r[:, a].reshape(ny * QROWS, zc) for a in range(mine)], axis=1)
    solved = product((ymat[0], ymat[1]), split(gathered))
    for q in range(ny):
        for a in range(mine):
            bs[q, a * own : (a + 1) * own] = solved[q * own : (q + 1) * own, a * zc : (a + 1) * zc]

    span = mine * own
    base = OVMAX * own

    def back(peer):
        return remote(
            bs.at[peer], rh.at[pl.ds(base + py * span, span)], bs_sem.at[peer], br_sem.at[py], (px, peer)
        )

    @pl.loop(1, ny)
    def _(d):
        back(lax.rem(py + d, ny)).start()

    rh[pl.ds(base + py * span, span)] = bs[py]

    @pl.loop(1, ny)
    def _(d):
        peer = lax.rem(py + d, ny)
        remote(
            bs.at[peer], rh.at[pl.ds(base + peer * span, span)], bs_sem.at[peer], br_sem.at[peer], (px, peer)
        ).wait()

    def margin_copy(side):
        size = OVMAX * own
        src = base if side == 0 else block * own
        dst = base + block * own if side == 0 else 0
        return remote(
            rh.at[pl.ds(src, size)], rh.at[pl.ds(dst, size)], hs_sem.at[side], hr_sem.at[1 - side], to[side]
        )

    def control_copy(side):
        src = HALO if side == 0 else block
        dst = HALO + block if side == 0 else 0
        return remote(
            ce.at[pl.ds(src, HALO)], ce.at[pl.ds(dst, HALO)], cs_sem.at[side], cr_sem.at[1 - side], to[side]
        )

    def exchange(make, arrive):
        for side in (0, 1):
            when_do(has[side], lambda side=side: make(side).start())
        for side in (0, 1):

            @pl.when(has[side])
            def _(side=side):
                make(side).wait_send()
                arrive(side).wait_recv()

    size = OVMAX * own
    exchange(
        margin_copy,
        lambda side: remote(
            rh.at[pl.ds(base, size)],
            rh.at[pl.ds(0 if side == 0 else base + block * own, size)],
            hs_sem.at[side],
            hr_sem.at[side],
            to[side],
        ),
    )
    kind = jnp.where(px == 0, 0, jnp.where(px == nx - 1, 2, 1))
    index = (kind * (OVMAX + 1) + margin[0, 0]) * (OVMAX + 1) + margin[0, 1]
    mats = tab[index]
    width = block + 2 * OVMAX
    right = jnp.concatenate([rh[pl.ds(m, width, stride=own), :] for m in range(own)], axis=1)
    first = product(split(mats[:block, :width]), split(right))
    ce[HALO : HALO + block] = first
    exchange(
        control_copy,
        lambda side: remote(
            ce.at[pl.ds(HALO, HALO)],
            ce.at[pl.ds(0 if side == 0 else HALO + block, HALO)],
            cs_sem.at[side],
            cr_sem.at[side],
            to[side],
        ),
    )
    second = product(split(mats[block:]), split(ce[...]))
    final = 2.0 * first - second
    for m in range(own):
        ctrl_out[pl.ds(m, block, stride=own), :] = final[:, m * zc : (m + 1) * zc]


def per_device(field, diffusivity, velocity, margin):
    cx, cy, nz = field.shape
    nx, ny = lax.axis_size("px"), lax.axis_size("py")
    chunks = 4
    block, own, zc = cx // 2, cy // 2, nz // 2
    mine = block // ny
    zmat = halves(z_matrix(nz))
    ymat = halves(y_matrix(cy * ny, ny))
    tab = jnp.asarray(schwarz_table(cx * nx, nx))
    f32, bf16 = jnp.float32, jnp.bfloat16
    V, D = pltpu.VMEM, pltpu.SemaphoreType.DMA
    slab = (cx, cy, nz)
    scratch = [
        V((2, cx + 2, cy, nz), f32),
        V(slab, bf16),
        V((3,) + slab, bf16),
        V((cx + 2, cy, nz), f32),
        V(slab, f32),
        V(slab, f32),
        V((cx + 2, cy, nz), f32),
        V(slab, f32),
        V(slab, f32),
        V((2, STEPS + 2, cx, nz), f32),
        V((2, STEPS + 2, cx, nz), f32),
        V((2, cx, nz), f32),
        V((2, cy, nz), bf16),
        V((2, cy, nz), bf16),
        V((2, 2, cy, nz), f32),
        V((2, 2, cy, nz), f32),
        V((block, cy, nz), f32),
        V((mine, cy + 24, zc), f32),
        V((ny, mine, QROWS, zc), f32),
        V((ny, mine, QROWS, zc), f32),
        V((ny, mine * own, zc), f32),
        V(((block + 2 * OVMAX) * own, zc), f32),
        V((block + 2 * HALO, own * zc), f32),
        V(zmat.shape, bf16),
        V(ymat.shape, bf16),
        V(tab.shape, f32),
        D((3,)),
        D((3,)),
        D((STEPS, 2)),
        D((STEPS, 2)),
        D((2, 2)),
        D((2, 2)),
        D((STEPS, chunks, 2)),
        D((STEPS, chunks, 2)),
        D((2,)),
        D((2,)),
        D((ny,)),
        D((ny,)),
        D((ny,)),
        D((ny,)),
        D((2,)),
        D((2,)),
        D((2,)),
        D((2,)),
    ]
    hbm = pl.BlockSpec(memory_space=pltpu.HBM)
    vmem = pl.BlockSpec(memory_space=pltpu.VMEM)
    adv, ctrl = pl.pallas_call(
        functools.partial(kernel, nx, ny, cx, cy, nz, chunks),
        out_shape=(
            jax.ShapeDtypeStruct(slab, f32),
            jax.ShapeDtypeStruct((block * own, zc), f32),
        ),
        in_specs=[pl.BlockSpec(memory_space=pltpu.SMEM)] + [hbm] * 6,
        out_specs=(vmem, vmem),
        scratch_shapes=scratch,
        compiler_params=pltpu.CompilerParams(
            collective_id=0, has_side_effects=True, vmem_limit_bytes=57 * 2**20
        ),
    )(margin, field, diffusivity, velocity, zmat, ymat, tab)
    return adv, ctrl.reshape(block, own, zc)


def solution(mesh):
    placed = (P("px", "py", None), P("px", "py", None), P(None, "px", "py", None), P("px", None))
    return jax.shard_map(
        per_device,
        mesh=mesh,
        in_specs=placed,
        out_specs=(P("px", "py", None), P("px", "py", None)),
        check_vma=False,
    )
```

```python
import functools

import jax
import jax.numpy as jnp
import numpy as np
from jax import lax
from jax.experimental import pallas as pl
from jax.experimental.pallas import tpu as pltpu
from jax.sharding import PartitionSpec as P

STEPS = 4
OVMAX = 4
HALO = 8
QROWS = 24
UNROLL = 4
MESH = pl.DeviceIdType.MESH


def bspline(t):
    t = np.abs(t)
    inner = (4.0 - 6.0 * t * t + 3.0 * t**3) / 6.0
    outer = np.maximum(2.0 - t, 0.0) ** 3 / 6.0
    return np.where(t < 1.0, inner, outer)


def basis(total):
    j = np.arange(total, dtype=np.float64)[:, None]
    k = np.arange(total // 2, dtype=np.float64)[None, :]
    return bspline(0.5 * (j - 2.0 * k - 0.5))


TAPS = [float(bspline(0.5 * (j - 3.5))) for j in range(8)]


def z_matrix(total):
    table = basis(total)
    return np.linalg.solve(table.T @ table, table.T).T.astype(np.float32)


def y_matrix(total, count):
    table = basis(total)
    inverse = np.linalg.inv(table.T @ table)
    ctrl = total // 2
    own = ctrl // count
    result = np.zeros((ctrl, count, QROWS))
    for p in range(count):
        for q in range(own + 4):
            k = own * p - 2 + q
            if 0 <= k < ctrl:
                result[:, p, q] = inverse[:, k]
    return result.reshape(ctrl, count * QROWS).astype(np.float32)


def schwarz_table(total, count):
    table = basis(total)
    gram = table.T @ table
    ctrl = total // 2
    block = ctrl // count
    width = block + 2 * OVMAX
    out = np.zeros((3, OVMAX + 1, OVMAX + 1, 2, block, block + 2 * HALO))
    for kind, p in enumerate((0, min(1, count - 1), count - 1)):
        start = p * block
        knots = start - OVMAX + np.arange(width)
        near = start - HALO + np.arange(block + 2 * HALO)

        def pick(rows, cols):
            good = ((rows >= 0) & (rows < ctrl))[:, None] & ((cols >= 0) & (cols < ctrl))[None, :]
            return np.where(good, gram[np.clip(rows, 0, ctrl - 1)][:, np.clip(cols, 0, ctrl - 1)], 0.0)

        full, rows = pick(knots, knots), pick(knots, near)
        for low in range(OVMAX + 1):
            for up in range(OVMAX + 1):
                weight = (knots >= start - low) & (knots < start + block + up) & (knots >= 0) & (knots < ctrl)
                weight = weight.astype(np.float64)
                local = full * weight[:, None] * weight[None, :] + np.diag(1.0 - weight)
                own = (np.linalg.inv(local) * weight[None, :])[OVMAX : OVMAX + block]
                out[kind, low, up, 0, :, :width] = own
                out[kind, low, up, 1] = own @ rows
    return out.reshape(-1, 2 * block, block + 2 * HALO).astype(np.float32)


def split(a):
    top = a.astype(jnp.bfloat16)
    return top, (a - top.astype(jnp.float32)).astype(jnp.bfloat16)


def product(a, b):
    dot = functools.partial(jnp.dot, preferred_element_type=jnp.float32)
    return dot(a[0], b[0]) + (dot(a[0], b[1]) + dot(a[1], b[0]))


def halves(a):
    top = a.astype(jnp.bfloat16)
    return jnp.asarray(np.stack([top, (a - top.astype(np.float32)).astype(jnp.bfloat16)]))


def kernel(
    nx, ny, cx, cy, nz, chunks,
    margin, field, kappa, velo, zmat_h, ymat_h, tab_h,
    adv_h, ctrl_out,
    adv, U, kb, vb, kk, ky, kz, hx, hy, hz, ys, yr, gy, kxr, hxr,
    xps, xpr, xc, zf, a2s, a2r, bs, rh, ce, zmat, ymat, tab,
    out_sem, in_sem, cst_sem, xs_sem, xr_sem, ki_s, ki_r, ys_sem, yr_sem, ps_sem, pr_sem,
    as_sem, ar_sem, bs_sem, br_sem, hs_sem, hr_sem, cs_sem, cr_sem,
):
    px, py = lax.axis_index("px"), lax.axis_index("py")
    rows = cx // chunks
    block = cx // 2
    mine = block // ny
    own = cy // 2
    zc = nz // 2

    loads = [
        pltpu.make_async_copy(kappa, kb, in_sem.at[0]),
        pltpu.make_async_copy(velo, vb, in_sem.at[1]),
        pltpu.make_async_copy(field, U.at[0, pl.ds(1, cx)], in_sem.at[2]),
    ]
    consts = [
        pltpu.make_async_copy(zmat_h, zmat, cst_sem.at[0]),
        pltpu.make_async_copy(ymat_h, ymat, cst_sem.at[1]),
        pltpu.make_async_copy(tab_h, tab, cst_sem.at[2]),
    ]
    for c in loads + consts:
        c.start()

    zero_face = jnp.zeros((cy, nz), jnp.float32)
    for s in range(2):
        U[s, 0] = zero_face
        U[s, cx + 1] = zero_face
        kxr[s] = jnp.zeros((cy, nz), kxr.dtype)
        hxr[s] = jnp.zeros((cy, nz), hxr.dtype)
        xpr[s] = jnp.zeros((2, cy, nz), jnp.float32)
    yr[...] = jnp.zeros(yr.shape, jnp.float32)
    rh[...] = jnp.zeros(rh.shape, jnp.float32)
    ce[0:HALO] = jnp.zeros((HALO, own * zc), jnp.float32)
    ce[HALO + block :] = jnp.zeros((HALO, own * zc), jnp.float32)
    zf[...] = jnp.zeros(zf.shape, jnp.float32)
    a2r[...] = jnp.zeros(a2r.shape, jnp.float32)

    barrier = pltpu.get_barrier_semaphore()

    @pl.loop(1, ny)
    def _(d):
        pl.semaphore_signal(barrier, inc=1, device_id=(px, lax.rem(py + d, ny)), device_id_type=MESH)

    has = {0: px > 0, 1: px < nx - 1}
    to = {0: (px - 1, py), 1: (px + 1, py)}
    hasy = {0: py > 0, 1: py < ny - 1}
    toy = {0: (px, py - 1), 1: (px, py + 1)}
    for side in (0, 1):

        @pl.when(has[side])
        def _(side=side):
            pl.semaphore_signal(barrier, inc=1, device_id=to[side], device_id_type=MESH)

    neighbours = jnp.where(px > 0, 1, 0) + jnp.where(px < nx - 1, 1, 0)
    pl.semaphore_wait(barrier, ny - 1 + neighbours)

    def remote(src, dst, ss, rs, dev):
        return pltpu.make_async_remote_copy(
            src_ref=src, dst_ref=dst, send_sem=ss, recv_sem=rs, device_id=dev, device_id_type=MESH
        )

    def x_init(side):
        edge = 0 if side == 0 else cx - 1
        return [
            remote(kappa.at[edge], kxr.at[1 - side], ki_s.at[0, side], ki_r.at[0, 1 - side], to[side]),
            remote(velo.at[0, edge], hxr.at[1 - side], ki_s.at[1, side], ki_r.at[1, 1 - side], to[side]),
            remote(
                field.at[edge],
                U.at[0, cx + 1 if side == 0 else 0],
                xs_sem.at[0, side],
                xr_sem.at[0, 1 - side],
                to[side],
            ),
        ]

    def x_face(t, side):
        slot = t % 2
        return remote(
            U.at[slot, 1 if side == 0 else cx],
            U.at[slot, cx + 1 if side == 0 else 0],
            xs_sem.at[t, side],
            xr_sem.at[t, 1 - side],
            to[side],
        )

    def y_face(t, c, side):
        items = pl.ds(0, 3) if t == 0 else pl.ds(t + 2, 1)
        part = pl.ds(c * rows, rows)
        return remote(
            ys.at[side, items, part],
            yr.at[1 - side, items, part],
            ys_sem.at[t, c, side],
            yr_sem.at[t, c, 1 - side],
            toy[side],
        )

    def y_arrival(t, c, side):
        items = pl.ds(0, 3) if t == 0 else pl.ds(t + 2, 1)
        part = pl.ds(c * rows, rows)
        return remote(
            ys.at[side, items, part],
            yr.at[side, items, part],
            ys_sem.at[t, c, side],
            yr_sem.at[t, c, side],
            toy[side],
        )

    def x_arrival(t, side):
        slot = t % 2
        return remote(
            U.at[slot, 1],
            U.at[slot, 0 if side == 0 else cx + 1],
            xs_sem.at[t, side],
            xr_sem.at[t, side],
            to[side],
        )

    def when_do(cond, do):
        pl.when(cond)(do)

    for side in (0, 1):

        @pl.when(has[side])
        def _(side=side):
            for c in x_init(side):
                c.start()

    for c in loads:
        c.wait()

    lane = lax.broadcasted_iota(jnp.int32, (cy, nz), 1)
    last_lane = lane == nz - 1

    def prepare(x):
        k = kb[x].astype(jnp.float32) * 0.05
        kk[x + 1] = k
        ky[x] = k + pltpu.roll(k, cy - 1, 0)
        kz[x] = k + jnp.where(last_lane, 0.0, pltpu.roll(k, nz - 1, 1))
        hx[x + 1] = vb[0, x].astype(jnp.float32) * 0.025
        h = vb[1, x].astype(jnp.float32) * 0.025
        hy[x] = h
        g = vb[2, x].astype(jnp.float32) * 0.025
        hz[x] = g
        u = U[0, x + 1]
        at = pl.ds(x, 1)
        for side, pick in ((0, slice(0, 1)), (1, slice(cy - 1, cy))):
            ys[side, 0, at] = k[pick]
            ys[side, 1, at] = h[pick]
            ys[side, 2, at] = u[pick]

    for c in range(chunks):

        @pl.loop(0, rows // UNROLL)
        def _(i, c=c):
            for r in range(UNROLL):
                prepare(c * rows + UNROLL * i + r)

        for side in (0, 1):
            when_do(hasy[side], lambda c=c, side=side: y_face(0, c, side).start())

    for side in (0, 1):

        @pl.when(has[side])
        def _(side=side):
            remote(kappa.at[0], kxr.at[side], ki_s.at[0, side], ki_r.at[0, side], to[side]).wait_recv()
            remote(velo.at[0, 0], hxr.at[side], ki_s.at[1, side], ki_r.at[1, side], to[side]).wait_recv()

        at = 0 if side == 0 else cx + 1
        kk[at] = kxr[side].astype(jnp.float32) * 0.05
        hx[at] = hxr[side].astype(jnp.float32) * 0.025

    tiles = [(slice(8 * i, 8 * i + 8), slice(128 * j, 128 * j + 128)) for i in range(cy // 8) for j in range(nz // 128)]
    high, wide = cy // 8, nz // 128
    trow = lax.broadcasted_iota(jnp.int32, (8, 128), 0)
    tlane = lax.broadcasted_iota(jnp.int32, (8, 128), 1)
    row_end, row_start = trow == 7, trow == 0
    lane_end, lane_start = tlane == 127, tlane == 0

    def x_start(s, x):
        flux, force = [], []
        for a, b in tiles:
            u, up = U[s, x, a, b], U[s, x + 1, a, b]
            fp = hx[x + 1, a, b] * (up * up)
            flux.append((kk[x, a, b] + kk[x + 1, a, b]) * (up - u) - (hx[x, a, b] * (u * u) + fp))
            force.append(fp)
        return tuple(flux), tuple(force)

    def partial(side):
        for q in range(2):
            k = (q - 2) if side == 0 else block + q
            total = None
            for j in range(8):
                i = 2 * k - 3 + j
                if 0 <= i < cx:
                    term = TAPS[j] * adv[i]
                    total = term if total is None else total + term
            xps[side, q] = total
        return remote(xps.at[side], xpr.at[1 - side], ps_sem.at[side], pr_sem.at[1 - side], to[side])

    order = [0, chunks - 1] + list(range(1, chunks - 1)) if chunks > 1 else [0]
    for t in range(STEPS):
        s = t % 2
        last = t == STEPS - 1
        for c in order:
            if c == 0:
                when_do(has[0], lambda t=t: x_arrival(t, 0).wait_recv())
            if c == chunks - 1:
                when_do(has[1], lambda t=t: x_arrival(t, 1).wait_recv())
            for side in (0, 1):
                when_do(hasy[side], lambda t=t, c=c, side=side: y_arrival(t, c, side).wait_recv())
            part = pl.ds(c * rows, rows)
            for side in (0, 1):
                a, b = ys[side, t + 2, part], yr[side, t + 2, part]
                diff = (a - b) if side == 0 else (b - a)
                gy[side, part] = (ys[side, 0, part] + yr[side, 0, part]) * diff - (
                    ys[side, 1, part] * (a * a) + yr[side, 1, part] * (b * b)
                )

            def line(x, carry, s=s):
                flux, force = carry
                at = pl.ds(x, 1)
                n = len(tiles)
                low_face, top_face = gy[0, at], gy[1, at]
                u = [U[s, x + 1, a, b] for a, b in tiles]
                sq = [v * v for v in u]
                gx, fx, new = [], [], []
                for m, (a, b) in enumerate(tiles):
                    up = U[s, x + 2, a, b]
                    fp = hx[x + 2, a, b] * (up * up)
                    g = (kk[x + 1, a, b] + kk[x + 2, a, b]) * (up - u[m]) - (force[m] + fp)
                    gx.append(g)
                    fx.append(fp)
                    new.append(u[m] + (g - flux[m]))
                ru = [pltpu.roll(v, 7, 0) for v in u]
                fy = [hy[x, a, b] * sq[m] for m, (a, b) in enumerate(tiles)]
                rf = [pltpu.roll(v, 7, 0) for v in fy]
                before = [None] * wide
                for m, (a, b) in enumerate(tiles):
                    j = m % wide
                    if m + wide < n:
                        up = jnp.where(row_end, ru[m + wide], ru[m])
                        fp = jnp.where(row_end, rf[m + wide], rf[m])
                    else:
                        up, fp = ru[m], rf[m]
                    g = ky[x, a, b] * (up - u[m]) - (fy[m] + fp)
                    if m + wide >= n:
                        g = jnp.where(row_end, top_face[:, b], g)
                    rg = pltpu.roll(g, 1, 0)
                    low = low_face[:, b] if m < wide else before[j]
                    new[m] = new[m] + (g - jnp.where(row_start, low, rg))
                    before[j] = rg
                for r in range(high):
                    fz = [hz[x, a, b] * sq[r * wide + j] for j, (a, b) in enumerate(tiles[r * wide : r * wide + wide])]
                    ru = [pltpu.roll(u[r * wide + j], 127, 1) for j in range(wide)]
                    rf = [pltpu.roll(v, 127, 1) for v in fz]
                    prev = None
                    for j in range(wide):
                        m = r * wide + j
                        a, b = tiles[m]
                        up = jnp.where(lane_end, ru[j + 1] if j + 1 < wide else 0.0, ru[j])
                        fp = jnp.where(lane_end, rf[j + 1] if j + 1 < wide else 0.0, rf[j])
                        g = kz[x, a, b] * (up - u[m]) - (fz[j] + fp)
                        rg = pltpu.roll(g, 1, 1)
                        low = kk[x + 1, a, b] * u[m] - fz[j] if j == 0 else prev
                        new[m] = new[m] + (g - jnp.where(lane_start, low, rg))
                        prev = rg
                return new, (tuple(gx), tuple(fx))

            def lines(i, carry, t=t, s=s, c=c, last=last):
                fresh = []
                for r in range(UNROLL):
                    x = c * rows + UNROLL * i + r
                    new, carry = line(x, carry)
                    fresh.append((x, new))
                for x, new in fresh:
                    at = pl.ds(x, 1)
                    for m, (a, b) in enumerate(tiles):
                        if last:
                            adv[x, a, b] = new[m]
                        else:
                            U[1 - s, x + 1, a, b] = new[m]
                    if not last:
                        ys[0, t + 3, at] = jnp.concatenate([v[0:1] for v in new[:wide]], axis=1)
                        ys[1, t + 3, at] = jnp.concatenate([v[7:8] for v in new[-wide:]], axis=1)
                return carry

            lax.fori_loop(0, rows // UNROLL, lines, x_start(s, c * rows))
            if not last:
                for side in (0, 1):
                    when_do(hasy[side], lambda t=t, c=c, side=side: y_face(t + 1, c, side).start())
                if c == 0:
                    when_do(has[0], lambda t=t: x_face(t + 1, 0).start())
                if c == chunks - 1:
                    when_do(has[1], lambda t=t: x_face(t + 1, 1).start())
            else:
                for side, at in ((0, 0), (1, chunks - 1)):
                    if c == at:
                        copy = partial(side)
                        when_do(has[side], lambda copy=copy: copy.start())
        for side in (0, 1):

            @pl.when(has[side])
            def _(t=t, side=side):
                x_face(t, side).wait_send()
                if t == 0:
                    for c in x_init(side)[:2]:
                        c.wait_send()

            @pl.when(hasy[side])
            def _(t=t, side=side):
                for c in range(chunks):
                    y_face(t, c, side).wait_send()

    leaving = pltpu.make_async_copy(adv, adv_h, out_sem.at[0])
    leaving.start()

    def x_row(k, low, high):
        total = None
        for j in range(8):
            if low <= j < high:
                term = TAPS[j] * adv[2 * k - 3 + j]
                total = term if total is None else total + term
        return total

    for k in (0, 1):
        xc[k] = x_row(k, 3 - 2 * k, 8)
    for k in (block - 2, block - 1):
        xc[k] = x_row(k, 0, cx - 2 * k + 3)

    @pl.loop(0, (block - 4) // UNROLL)
    def _(i):
        for r in range(UNROLL):
            k = 2 + UNROLL * i + r
            xc[k] = x_row(k, 0, 8)

    for side in (0, 1):

        @pl.when(has[side])
        def _(side=side):
            c = remote(xps.at[side], xpr.at[side], ps_sem.at[side], pr_sem.at[side], to[side])
            c.wait()

        for q in range(2):
            k = q if side == 0 else block - 2 + q
            xc[k] += xpr[side, q]

    for c in consts:
        c.wait()

    def group(peer):
        first = peer * mine
        lines = xc[pl.ds(first, mine)].reshape(mine * cy, nz)
        fitted = product(split(lines), (zmat[0], zmat[1]))
        zf[:, 8 : 8 + cy, :] = fitted.reshape(mine, cy, zc)
        for a in range(mine):
            total = None
            for j in range(8):
                term = TAPS[j] * zf[a, pl.ds(1 + j, QROWS, stride=2), :]
                total = term if total is None else total + term
            a2s[peer, a] = total

    used = pl.ds(0, own + 4)

    def a2a(peer):
        return remote(a2s.at[peer, :, used], a2r.at[py, :, used], as_sem.at[peer], ar_sem.at[py], (px, peer))

    @pl.loop(1, ny)
    def _(d):
        peer = lax.rem(py + d, ny)
        group(peer)
        a2a(peer).start()

    group(py)
    a2r[py] = a2s[py]

    @pl.loop(1, ny)
    def _(d):
        peer = lax.rem(py + d, ny)
        remote(a2s.at[peer, :, used], a2r.at[peer, :, used], as_sem.at[peer], ar_sem.at[peer], (px, peer)).wait()

    gathered = jnp.concatenate([a2r[:, a].reshape(ny * QROWS, zc) for a in range(mine)], axis=1)
    solved = product((ymat[0], ymat[1]), split(gathered))
    for q in range(ny):
        for a in range(mine):
            bs[q, a * own : (a + 1) * own] = solved[q * own : (q + 1) * own, a * zc : (a + 1) * zc]

    span = mine * own
    base = OVMAX * own

    def back(peer):
        return remote(
            bs.at[peer], rh.at[pl.ds(base + py * span, span)], bs_sem.at[peer], br_sem.at[py], (px, peer)
        )

    @pl.loop(1, ny)
    def _(d):
        back(lax.rem(py + d, ny)).start()

    rh[pl.ds(base + py * span, span)] = bs[py]

    @pl.loop(1, ny)
    def _(d):
        peer = lax.rem(py + d, ny)
        remote(
            bs.at[peer], rh.at[pl.ds(base + peer * span, span)], bs_sem.at[peer], br_sem.at[peer], (px, peer)
        ).wait()

    def margin_copy(side):
        size = OVMAX * own
        src = base if side == 0 else block * own
        dst = base + block * own if side == 0 else 0
        return remote(
            rh.at[pl.ds(src, size)], rh.at[pl.ds(dst, size)], hs_sem.at[side], hr_sem.at[1 - side], to[side]
        )

    def control_copy(side):
        src = HALO if side == 0 else block
        dst = HALO + block if side == 0 else 0
        return remote(
            ce.at[pl.ds(src, HALO)], ce.at[pl.ds(dst, HALO)], cs_sem.at[side], cr_sem.at[1 - side], to[side]
        )

    def exchange(make, arrive):
        for side in (0, 1):
            when_do(has[side], lambda side=side: make(side).start())
        for side in (0, 1):

            @pl.when(has[side])
            def _(side=side):
                make(side).wait_send()
                arrive(side).wait_recv()

    size = OVMAX * own
    exchange(
        margin_copy,
        lambda side: remote(
            rh.at[pl.ds(base, size)],
            rh.at[pl.ds(0 if side == 0 else base + block * own, size)],
            hs_sem.at[side],
            hr_sem.at[side],
            to[side],
        ),
    )
    kind = jnp.where(px == 0, 0, jnp.where(px == nx - 1, 2, 1))
    index = (kind * (OVMAX + 1) + margin[0, 0]) * (OVMAX + 1) + margin[0, 1]
    mats = tab[index]
    width = block + 2 * OVMAX
    right = jnp.concatenate([rh[pl.ds(m, width, stride=own), :] for m in range(own)], axis=1)
    first = product(split(mats[:block, :width]), split(right))
    ce[HALO : HALO + block] = first
    exchange(
        control_copy,
        lambda side: remote(
            ce.at[pl.ds(HALO, HALO)],
            ce.at[pl.ds(0 if side == 0 else HALO + block, HALO)],
            cs_sem.at[side],
            cr_sem.at[side],
            to[side],
        ),
    )
    second = product(split(mats[block:]), split(ce[...]))
    final = 2.0 * first - second
    leaving.wait()
    for m in range(own):
        ctrl_out[pl.ds(m, block, stride=own), :] = final[:, m * zc : (m + 1) * zc]


def per_device(field, diffusivity, velocity, margin):
    cx, cy, nz = field.shape
    nx, ny = lax.axis_size("px"), lax.axis_size("py")
    chunks = 4
    assert cx % (chunks * UNROLL) == 0 and (cx // 2 - 4) % UNROLL == 0
    block, own, zc = cx // 2, cy // 2, nz // 2
    mine = block // ny
    zmat = halves(z_matrix(nz))
    ymat = halves(y_matrix(cy * ny, ny))
    tab = jnp.asarray(schwarz_table(cx * nx, nx))
    f32, bf16 = jnp.float32, jnp.bfloat16
    V, D = pltpu.VMEM, pltpu.SemaphoreType.DMA
    slab = (cx, cy, nz)
    scratch = [
        V(slab, f32),
        V((2, cx + 2, cy, nz), f32),
        V(slab, bf16),
        V((3,) + slab, bf16),
        V((cx + 2, cy, nz), f32),
        V(slab, f32),
        V(slab, f32),
        V((cx + 2, cy, nz), f32),
        V(slab, f32),
        V(slab, f32),
        V((2, STEPS + 2, cx, nz), f32),
        V((2, STEPS + 2, cx, nz), f32),
        V((2, cx, nz), f32),
        V((2, cy, nz), bf16),
        V((2, cy, nz), bf16),
        V((2, 2, cy, nz), f32),
        V((2, 2, cy, nz), f32),
        V((block, cy, nz), f32),
        V((mine, cy + 24, zc), f32),
        V((ny, mine, QROWS, zc), f32),
        V((ny, mine, QROWS, zc), f32),
        V((ny, mine * own, zc), f32),
        V(((block + 2 * OVMAX) * own, zc), f32),
        V((block + 2 * HALO, own * zc), f32),
        V(zmat.shape, bf16),
        V(ymat.shape, bf16),
        V(tab.shape, f32),
        D((1,)),
        D((3,)),
        D((3,)),
        D((STEPS, 2)),
        D((STEPS, 2)),
        D((2, 2)),
        D((2, 2)),
        D((STEPS, chunks, 2)),
        D((STEPS, chunks, 2)),
        D((2,)),
        D((2,)),
        D((ny,)),
        D((ny,)),
        D((ny,)),
        D((ny,)),
        D((2,)),
        D((2,)),
        D((2,)),
        D((2,)),
    ]
    hbm = pl.BlockSpec(memory_space=pltpu.HBM)
    vmem = pl.BlockSpec(memory_space=pltpu.VMEM)
    adv, ctrl = pl.pallas_call(
        functools.partial(kernel, nx, ny, cx, cy, nz, chunks),
        out_shape=(
            jax.ShapeDtypeStruct(slab, f32),
            jax.ShapeDtypeStruct((block * own, zc), f32),
        ),
        in_specs=[pl.BlockSpec(memory_space=pltpu.SMEM)] + [hbm] * 6,
        out_specs=(hbm, vmem),
        scratch_shapes=scratch,
        compiler_params=pltpu.CompilerParams(
            collective_id=0, has_side_effects=True, vmem_limit_bytes=57 * 2**20
        ),
    )(margin, field, diffusivity, velocity, zmat, ymat, tab)
    return adv, ctrl.reshape(block, own, zc)


def solution(mesh):
    placed = (P("px", "py", None), P("px", "py", None), P(None, "px", "py", None), P("px", None))
    return jax.shard_map(
        per_device,
        mesh=mesh,
        in_specs=placed,
        out_specs=(P("px", "py", None), P("px", "py", None)),
        check_vma=False,
    )
```
